32 devices in a mesh: dp: 2 (over x), row: 4 (over y, core), col: 4 (over z).
Axes of the slice: x: 2, y: 2, z: 4, core: 2. Of those that a mesh axis runs over, the one named last changes fastest.
Arguments:
- stream: bfloat16 [3072, 1536], P(('dp', 'col'), 'row'), may hold values from -6 to 6
- cotangent: bfloat16 [3072, 1536], P(('dp', 'col'), 'row'), may hold values from -6 to 6
- first_gain: float32 [1536], P('row'), may hold values from 0.25 to 1.75
- query_weight: bfloat16 [1536, 1536], P('row', 'col'), may hold values from -0.15625 to 0.15625
- query_bias: float32 [1536], P('col'), may hold values from -3 to 3
- key_weight: bfloat16 [1536, 256], P('row'), may hold values from -0.15625 to 0.15625
- key_bias: float32 [256], replicated, may hold values from -3 to 3
- value_weight: bfloat16 [1536, 256], P('row'), may hold values from -0.15625 to 0.15625
- value_bias: float32 [256], replicated, may hold values from -3 to 3
- output_weight: bfloat16 [1536, 1536], P('col', 'row'), may hold values from -0.625 to 0.625
- second_gain: float32 [1536], P('row'), may hold values from 0.25 to 1.75
- gate_weight: bfloat16 [1536, 8960], P('row', 'col'), may hold values from -0.15625 to 0.15625
- up_weight: bfloat16 [1536, 8960], P('row', 'col'), may hold values from -0.15625 to 0.15625
- down_weight: bfloat16 [8960, 1536], P('col', 'row'), may hold values from -0.0625 to 0.0625
- seq_units: int32 [2, 4], P('dp'), may hold values from 1 to 7, 12 in all within a row
Outputs:
- block_out: bfloat16 [3072, 1536], P(('dp', 'col'), 'row')
- input_grad: bfloat16 [3072, 1536], P(('dp', 'col'), 'row')
- first_gain_grad: float32 [1536], P('row')
- query_weight_grad: float32 [1536, 1536], P('row', 'col')
- query_bias_grad: float32 [1536], P('col')
- key_weight_grad: float32 [1536, 256], P('row')
- key_bias_grad: float32 [256], replicated
- value_weight_grad: float32 [1536, 256], P('row')
- value_bias_grad: float32 [256], replicated
- output_weight_grad: float32 [1536, 1536], P('col', 'row')
- second_gain_grad: float32 [1536], P('row')
- gate_weight_grad: float32 [1536, 8960], P('row', 'col')
- up_weight_grad: float32 [1536, 8960], P('row', 'col')
- down_weight_grad: float32 [8960, 1536], P('col', 'row')
The draws below stay inside these ranges and needn't reach their ends.
Inputs may be any that keep to these rules, and one draw needn't show every extreme that they name: `seq_units`: row d lists in order the lengths, in units of 128 tokens, of the sequences packed into data shard d; each row sums to 12 and its largest entry is 7.
All inputs are finite; a program needn't handle non-finite values.
Results may differ from the reference program's by a relative error of at most 0.035.
Values may be sent and summed in bfloat16 or wider, within the bound.
No kernel may reach another device: no remote copies, remote signals or barrier semaphores. Data moves between devices by JAX's collectives and lax.ppermute only.
A program may use at most 192 MiB of HBM per device.

```python
import math
import jax
import jax.numpy as jnp
import numpy as np
from jax import lax

D = 1536
FF = 8960
QUERY_HEADS = 12
KEY_VALUE_HEADS = 2
HEAD_WIDTH = 128
UNIT = 128
TOKENS_PER_SHARD = 1536
TOKENS = 3072
KV = 256
HEADS_DEV = 3
SEQ_MAX = 896
NSEQ = 4
QB = 384
SPAN = 1280
N_DP = 2


def shard_levels(rng, extent, shards, smallest, largest):
    def one(dim, shards_of):
        heights = jax.random.uniform(jax.random.fold_in(jax.random.fold_in(rng, 6), dim), (shards_of,), jnp.float32, smallest / len(shards), largest / len(shards))
        return jnp.repeat(jnp.exp(heights), extent[dim] // shards_of).reshape((-1,) + (1,) * (len(extent) - dim - 1))

    factor_of = one(*shards[0])
    for cut in shards[1:]:
        factor_of = factor_of * one(*cut)
    return factor_of


def profile(amount, total, limit, slope):
    weights = [(1 << 20) // math.isqrt(standing ** slope) + 1 for standing in range(2, amount + 1)]
    rest, given = total - limit - (amount - 1), [1] * (amount - 1)
    while rest > 0:
        movable = [i for i in range(amount - 1) if given[i] < limit]
        mass, remaining = sum([weights[i] for i in movable]), rest
        for i in movable:
            extra = min(limit - given[i], max(1, remaining * weights[i] // mass), rest)
            given[i] = given[i] + extra
            rest = rest - extra
    return np.array([limit] + given)


def uneven(rng, number_of, total, bound, slope):
    if number_of == 2:
        one = jax.random.randint(rng, (), max(1, total - bound), min(bound, total - 1) + 1)
        return jnp.stack([one, total - one])
    sizes = jnp.asarray(profile(number_of, total, bound, slope), jnp.int32)
    couples = (number_of - 1) // 2
    source_of, sink = sizes[1:1 + 2 * couples:2], sizes[2:2 + 2 * couples:2]
    margin = jnp.minimum(source_of - 1, bound - sink)
    moved = jax.random.randint(jax.random.fold_in(rng, 1), (couples,), 0, 1 << 20) % (margin + 1)
    sizes = sizes.at[1:1 + 2 * couples:2].set(source_of - moved).at[2:2 + 2 * couples:2].set(sink + moved)
    return sizes[jax.random.permutation(jax.random.fold_in(rng, 2), number_of)]


def gaussian(stream_key, extent, deviation, bound, split=(), kind=jnp.bfloat16):
    factor_of = shard_levels(stream_key, extent, split, -0.22, 0.18) if split else 1.0
    entries = jax.random.normal(stream_key, extent, jnp.float32) * deviation * factor_of
    return jnp.minimum(jnp.maximum(entries, -bound), bound).astype(kind)


def setup_inputs(seed: int = 0) -> dict:
    keys = jax.random.split(jax.random.key(seed), 16)
    return {
        "stream": gaussian(keys[0], (TOKENS, D), 1.0, 6.0, ((0, 8), (1, 4))),
        "cotangent": gaussian(keys[1], (TOKENS, D), 1.0, 6.0, ((0, 8), (1, 4))),
        "first_gain": jnp.clip(1.0 + 0.15 * jax.random.normal(keys[2], (D,), jnp.float32), 0.25, 1.75),
        "query_weight": gaussian(keys[3], (D, D), D ** -0.5, 0.15625, ((0, 4), (1, 4))),
        "query_bias": gaussian(keys[4], (D,), 0.5, 3.0, ((0, 4),), jnp.float32),
        "key_weight": gaussian(keys[5], (D, KV), D ** -0.5, 0.15625, ((0, 4),)),
        "key_bias": gaussian(keys[6], (KV,), 0.5, 3.0, (), jnp.float32),
        "value_weight": gaussian(keys[7], (D, KV), D ** -0.5, 0.15625, ((0, 4),)),
        "value_bias": gaussian(keys[8], (KV,), 0.5, 3.0, (), jnp.float32),
        "output_weight": gaussian(keys[9], (D, D), (D // 16) ** -0.5, 0.625, ((0, 4), (1, 4))),
        "second_gain": jnp.clip(1.0 + 0.15 * jax.random.normal(keys[10], (D,), jnp.float32), 0.25, 1.75),
        "gate_weight": gaussian(keys[11], (D, FF), D ** -0.5, 0.15625, ((0, 4), (1, 4))),
        "up_weight": gaussian(keys[12], (D, FF), D ** -0.5, 0.15625, ((0, 4), (1, 4))),
        "down_weight": gaussian(keys[13], (FF, D), FF ** -0.5, 0.0625, ((0, 4), (1, 4))),
        "seq_units": jax.vmap(lambda own: uneven(own, NSEQ, TOKENS_PER_SHARD // UNIT, SEQ_MAX // UNIT, 1))(jax.random.split(keys[14], N_DP)).reshape((N_DP, NSEQ)).astype(jnp.int32),
    }


epsilon = 1e-06
rope_base = 1000000.0
neg_large = -1e+30

def matmul(left, right):
    return jnp.dot(left, right, preferred_element_type=jnp.float32)

def widen(values):
    return lax.optimization_barrier(values).astype(jnp.float32)

def rotate_half(values, position, direction):
    half_width = values.shape[-1] // 2
    frequency = rope_base ** (-jnp.arange(half_width, dtype=jnp.float32) / half_width)
    angle = position.astype(jnp.float32)[:, None] * frequency[None, :]
    cosine = jnp.cos(angle)[:, None, :]
    sine_part = direction * jnp.sin(angle)[:, None, :]
    leading = values[..., :half_width]
    trailing = values[..., half_width:]
    return jnp.concatenate([leading * cosine - trailing * sine_part, trailing * cosine + leading * sine_part], axis=-1)

def sequence_layout(unit_counts, length):
    lengths = (unit_counts * UNIT).astype(jnp.int32)
    seq_ends = jnp.cumsum(lengths).astype(jnp.int32)
    seq_starts = seq_ends - lengths
    places = jnp.arange(length, dtype=jnp.int32)
    segment = lax.optimization_barrier(jnp.sum((places[:, None] >= seq_ends[None, :]).astype(jnp.int32), axis=1)).astype(jnp.int32)
    member = segment[:, None] == jnp.arange(unit_counts.shape[0], dtype=jnp.int32)[None, :]
    begins = lax.optimization_barrier(jnp.sum(jnp.where(member, seq_starts[None, :], 0), axis=1)).astype(jnp.int32)
    return (segment, places - begins)

def block_mask(segment, query_first, window_first, query_rows, key_span):
    query_place = query_first + jnp.arange(query_rows, dtype=jnp.int32)
    key_place = window_first + jnp.arange(key_span, dtype=jnp.int32)
    query_seg = lax.dynamic_slice_in_dim(segment, query_first, query_rows, 0)
    key_seg = lax.dynamic_slice_in_dim(segment, window_first, key_span, 0)
    return (query_seg[:, None] == key_seg[None, :]) & (key_place[None, :] <= query_place[:, None])

def norm_backward(normed_grad, source, inv_scale, gain_vec):
    unit_rows = source * inv_scale[:, None]
    unit_grad = normed_grad * gain_vec[None, :]
    inner_mean = lax.optimization_barrier(jnp.mean(unit_grad * unit_rows, axis=1))
    return (inv_scale[:, None] * (unit_grad - unit_rows * inner_mean[:, None]), lax.optimization_barrier(jnp.sum(normed_grad * unit_rows, axis=0)))

def shard_pass(stream, cotangent, unit_counts, params):
    first_gain, query_weight, query_bias, key_weight, key_bias, value_weight, value_bias, output_weight, second_gain, gate_weight, up_weight, down_weight = params
    group_width = QUERY_HEADS // KEY_VALUE_HEADS
    parts_count = QUERY_HEADS // HEADS_DEV
    scale_qk = HEAD_WIDTH ** (-0.5)
    block_count = TOKENS_PER_SHARD // QB
    source = stream.astype(jnp.float32)
    first_scale = lax.rsqrt(lax.optimization_barrier(jnp.mean(source * source, axis=1)) + epsilon)
    first_normed = (source * first_scale[:, None] * first_gain[None, :]).astype(jnp.bfloat16)
    segment, start_shift = sequence_layout(unit_counts, TOKENS_PER_SHARD)
    queries = matmul(first_normed, query_weight) + query_bias[None, :]
    every_key = matmul(first_normed, key_weight) + key_bias[None, :]
    every_value = matmul(first_normed, value_weight) + value_bias[None, :]
    queries = rotate_half(queries.reshape(TOKENS_PER_SHARD, QUERY_HEADS, HEAD_WIDTH), start_shift, 1.0).astype(jnp.bfloat16)
    every_key = rotate_half(every_key.reshape(TOKENS_PER_SHARD, KEY_VALUE_HEADS, HEAD_WIDTH), start_shift, 1.0).astype(jnp.bfloat16)
    every_value = every_value.reshape(TOKENS_PER_SHARD, KEY_VALUE_HEADS, HEAD_WIDTH).astype(jnp.bfloat16)

    def window(block_index):
        query_first = block_index * QB
        window_first = min(max(query_first - SEQ_MAX, 0), TOKENS_PER_SHARD - SPAN)
        query_slab = widen(queries[query_first:query_first + QB])
        key_slab = widen(jnp.repeat(every_key[window_first:window_first + SPAN], group_width, axis=1))
        value_slab = widen(jnp.repeat(every_value[window_first:window_first + SPAN], group_width, axis=1))
        scores = jnp.einsum('qhd,khd->hqk', query_slab, key_slab) * scale_qk
        scores = jnp.where(block_mask(segment, query_first, window_first, QB, SPAN)[None], scores, neg_large)
        return (query_first, window_first, query_slab, key_slab, value_slab, scores)
    attn_parts = []
    log_parts = []
    for block_index in range(block_count):
        query_first, window_first, query_slab, key_slab, value_slab, scores = window(block_index)
        row_peak = lax.optimization_barrier(jnp.max(scores, axis=2))
        log_total = row_peak + jnp.log(lax.optimization_barrier(jnp.sum(jnp.exp(scores - row_peak[..., None]), axis=2)))
        attn_probs = jnp.exp(scores - log_total[..., None]).astype(jnp.bfloat16)
        mixed = jnp.einsum('hqk,khd->qhd', widen(attn_probs), value_slab)
        attn_parts.append(mixed.astype(jnp.bfloat16).reshape(QB, D))
        log_parts.append(log_total)
    attended = jnp.concatenate(attn_parts, axis=0)
    second = source + matmul(attended, output_weight)
    second_scale = lax.rsqrt(lax.optimization_barrier(jnp.mean(second * second, axis=1)) + epsilon)
    second_normed = (second * second_scale[:, None] * second_gain[None, :]).astype(jnp.bfloat16)
    gate_pre = matmul(second_normed, gate_weight)
    up_pre = matmul(second_normed, up_weight)
    hidden = (jax.nn.silu(gate_pre) * up_pre).astype(jnp.bfloat16)
    block_out = (second + matmul(hidden, down_weight)).astype(jnp.bfloat16)
    out_grad = cotangent.astype(jnp.float32)
    down_weight_grad = matmul(hidden.T, cotangent)
    hidden_grad = matmul(cotangent, down_weight.T)
    sigma = jax.nn.sigmoid(gate_pre)
    gate_grad = (hidden_grad * up_pre * sigma * (1.0 + gate_pre * (1.0 - sigma))).astype(jnp.bfloat16)
    up_grad = (hidden_grad * gate_pre * sigma).astype(jnp.bfloat16)
    gate_weight_grad = matmul(second_normed.T, gate_grad)
    up_weight_grad = matmul(second_normed.T, up_grad)
    second_normed_grad = matmul(gate_grad, gate_weight.T) + matmul(up_grad, up_weight.T)
    second_path, second_gain_grad = norm_backward(second_normed_grad, second, second_scale, second_gain)
    second_grad = out_grad + second_path
    mixed_cot = second_grad.astype(jnp.bfloat16)
    output_weight_grad = matmul(attended.T, mixed_cot)
    attended_grad = matmul(mixed_cot, output_weight.T).astype(jnp.bfloat16)
    key_acc = jnp.zeros((TOKENS_PER_SHARD, parts_count, HEAD_WIDTH), jnp.float32)
    value_acc = jnp.zeros((TOKENS_PER_SHARD, parts_count, HEAD_WIDTH), jnp.float32)
    query_parts = []
    for block_index in range(block_count):
        query_first, window_first, query_slab, key_slab, value_slab, scores = window(block_index)
        prob_full = jnp.exp(scores - log_parts[block_index][..., None])
        out_slab = widen(attended_grad[query_first:query_first + QB].reshape(QB, QUERY_HEADS, HEAD_WIDTH))
        attn_slab = widen(attended[query_first:query_first + QB].reshape(QB, QUERY_HEADS, HEAD_WIDTH))
        value_term = jnp.einsum('hqk,qhd->khd', widen(prob_full.astype(jnp.bfloat16)), out_slab)
        value_term = lax.optimization_barrier(jnp.sum(value_term.reshape(SPAN, parts_count, HEADS_DEV, HEAD_WIDTH), axis=2))
        prob_grad = jnp.einsum('qhd,khd->hqk', out_slab, value_slab)
        delta_row = lax.optimization_barrier(jnp.sum(out_slab * attn_slab, axis=2))
        score_grad = (prob_full * (prob_grad - jnp.transpose(delta_row)[:, :, None]) * scale_qk).astype(jnp.bfloat16)
        score_grad = widen(score_grad)
        query_parts.append(jnp.einsum('hqk,khd->qhd', score_grad, key_slab))
        key_term = jnp.einsum('hqk,qhd->khd', score_grad, query_slab)
        key_term = lax.optimization_barrier(jnp.sum(key_term.reshape(SPAN, parts_count, HEADS_DEV, HEAD_WIDTH), axis=2))
        key_acc = key_acc.at[window_first:window_first + SPAN].add(key_term)
        value_acc = value_acc.at[window_first:window_first + SPAN].add(value_term)
    query_grad = rotate_half(jnp.concatenate(query_parts, axis=0), start_shift, -1.0).reshape(TOKENS_PER_SHARD, D).astype(jnp.bfloat16)
    key_grad = rotate_half(key_acc, start_shift, -1.0).astype(jnp.bfloat16)
    value_grad = value_acc.astype(jnp.bfloat16)
    query_weight_grad = matmul(first_normed.T, query_grad)
    query_bias_grad = lax.optimization_barrier(jnp.sum(query_grad.astype(jnp.float32), axis=0))
    first_normed_grad = matmul(query_grad, query_weight.T)
    key_weight_grad = jnp.zeros((D, KV), jnp.float32)
    value_weight_grad = jnp.zeros((D, KV), jnp.float32)
    key_bias_grad = jnp.zeros((KV,), jnp.float32)
    value_bias_grad = jnp.zeros((KV,), jnp.float32)
    for part_index in range(parts_count):
        first_key_value = part_index * HEADS_DEV // group_width * HEAD_WIDTH
        key_piece = key_grad[:, part_index]
        value_piece = value_grad[:, part_index]
        key_weight_grad = key_weight_grad.at[:, first_key_value:first_key_value + HEAD_WIDTH].add(matmul(first_normed.T, key_piece))
        value_weight_grad = value_weight_grad.at[:, first_key_value:first_key_value + HEAD_WIDTH].add(matmul(first_normed.T, value_piece))
        key_bias_grad = key_bias_grad.at[first_key_value:first_key_value + HEAD_WIDTH].add(lax.optimization_barrier(jnp.sum(key_piece.astype(jnp.float32), axis=0)))
        value_bias_grad = value_bias_grad.at[first_key_value:first_key_value + HEAD_WIDTH].add(lax.optimization_barrier(jnp.sum(value_piece.astype(jnp.float32), axis=0)))
        first_normed_grad = first_normed_grad + matmul(key_piece, key_weight[:, first_key_value:first_key_value + HEAD_WIDTH].T)
        first_normed_grad = first_normed_grad + matmul(value_piece, value_weight[:, first_key_value:first_key_value + HEAD_WIDTH].T)
    first_path, first_gain_grad = norm_backward(first_normed_grad, source, first_scale, first_gain)
    input_grad = (second_grad + first_path).astype(jnp.bfloat16)
    grads = (first_gain_grad, query_weight_grad, query_bias_grad, key_weight_grad, key_bias_grad, value_weight_grad, value_bias_grad, output_weight_grad, second_gain_grad, gate_weight_grad, up_weight_grad, down_weight_grad)
    return (block_out, input_grad, grads)

def reference(stream, cotangent, first_gain, query_weight, query_bias, key_weight, key_bias, value_weight, value_bias, output_weight, second_gain, gate_weight, up_weight, down_weight, seq_units):
    params = (first_gain, query_weight, query_bias, key_weight, key_bias, value_weight, value_bias, output_weight, second_gain, gate_weight, up_weight, down_weight)
    shard_inputs = (stream.reshape(N_DP, TOKENS_PER_SHARD, D), cotangent.reshape(N_DP, TOKENS_PER_SHARD, D), seq_units)
    carry_init = tuple((jnp.zeros(tensor.shape, jnp.float32) for tensor in params))

    def step_shard(carry, inputs):
        block_out, input_grad, grads = shard_pass(inputs[0], inputs[1], inputs[2], params)
        return (tuple((held + fresh for held, fresh in zip(carry, grads))), (block_out, input_grad))
    totals, outputs = lax.scan(step_shard, carry_init, shard_inputs)
    block_out = outputs[0].reshape(TOKENS, D)
    input_grad = outputs[1].reshape(TOKENS, D)
    return (block_out, input_grad, totals[0], totals[1], totals[2], totals[3], totals[4], totals[5], totals[6], totals[7], totals[8], totals[9], totals[10], totals[11])
```

```python
import jax
import jax.numpy as jnp
from jax import lax
from jax.sharding import PartitionSpec as P

QUERY_HEADS = 12
KEY_VALUE_HEADS = 2
HEAD_WIDTH = 128
UNIT = 128
N = 4

epsilon = 1e-06
rope_base = 1000000.0
neg_large = -1e30
bf16 = jnp.bfloat16
f32 = jnp.float32


def rowx(a, j):
    return lax.ppermute(a, "row", [(i, i ^ j) for i in range(N)])


def zshift(a, s):
    return lax.ppermute(a, "col", [(i, (i + s) % N) for i in range(N)])


def zstep(a, s):
    return lax.ppermute(a, "col", [(i, i + s) for i in range(N) if 0 <= i + s < N])


def row_gather(a):
    c = rowx(a, 1)
    y = rowx(a, 2)
    return [a, c, y, rowx(y, 1)]


def row_scatter(parts):
    q0 = parts[0].astype(f32) + rowx(parts[1], 1).astype(f32)
    q2 = parts[2].astype(f32) + rowx(parts[3], 1).astype(f32)
    return q0 + rowx(q2.astype(bf16), 2).astype(f32)


def col_gather(a):
    z1 = zshift(a, 1)
    z3 = zshift(a, -1)
    return [a, z1, zshift(z1, 1), z3]


def col_scatter(parts):
    far = zshift(parts[2], -1)
    near = zshift(parts[3], 1)
    one = (parts[1].astype(f32) + far.astype(f32)).astype(bf16)
    return parts[0].astype(f32) + near.astype(f32) + zshift(one, -1).astype(f32)


def row_exchange(pick):
    return [pick(0)] + [rowx(pick(j), j) for j in range(1, N)]


def xor_order(blocks, core, yy):
    a = [jnp.where(core == 1, blocks[i ^ 1], blocks[i]) for i in range(N)]
    return [jnp.where(yy == 1, a[i ^ 2], a[i]) for i in range(N)]


def diagonal_gather(a, row, col):
    out = []
    for i in range(N):
        if i == 0:
            t = jnp.where(row == col, a, jnp.zeros_like(a))
        else:
            t = lax.ppermute(a, ("row", "col"), [(c * N + (c - i) % N, c * N + c) for c in range(N)])
        y = lax.ppermute(t, ("row", "col"), [(c * N + c, (c ^ 2) * N + c) for c in range(N)])
        t = t + y
        pairs = [(c * N + c, (c ^ 1) * N + c) for c in range(N)]
        pairs += [((c ^ 2) * N + c, (c ^ 3) * N + c) for c in range(N)]
        k = lax.ppermute(t, ("row", "col"), pairs)
        out.append(t + k)
    return out


def dp_sum(a):
    if lax.axis_size("dp") == 2:
        b = a.astype(bf16)
        return b.astype(f32) + lax.ppermute(b, "dp", [(0, 1), (1, 0)]).astype(f32)
    return lax.psum(a.astype(bf16), "dp").astype(f32)


def dot(a, b, ca, cb):
    return lax.dot_general(a, b, (((ca,), (cb,)), ((), ())), preferred_element_type=f32)


def rotate(values, cosine, sine):
    half = values.shape[-1] // 2
    a = values[..., :half]
    b = values[..., half:]
    return jnp.concatenate([a * cosine - b * sine, b * cosine + a * sine], axis=-1)


def layout_of(places, unit_counts):
    ends = jnp.cumsum(unit_counts * UNIT)
    starts = ends - unit_counts * UNIT
    seg = jnp.sum((places[:, None] >= ends[None, :]).astype(jnp.int32), axis=1)
    member = seg[:, None] == jnp.arange(unit_counts.shape[0], dtype=jnp.int32)[None, :]
    begin = jnp.sum(jnp.where(member, starts[None, :], 0), axis=1)
    return seg, places - begin


def local(
    stream,
    cotangent,
    first_gain,
    query_weight,
    query_bias,
    key_weight,
    key_bias,
    value_weight,
    value_bias,
    output_weight,
    second_gain,
    gate_weight,
    up_weight,
    down_weight,
    seq_units,
):
    row = lax.axis_index("row")
    col = lax.axis_index("col")
    rep = lax.axis_index("dp")
    n_dp = lax.axis_size("dp")
    core = row % 2
    yy = row // 2
    tok, feat = stream.shape
    width = feat * N
    heads = query_weight.shape[1] // HEAD_WIDTH
    hidden_width = gate_weight.shape[1]
    slice_width = hidden_width // N
    scale_qk = HEAD_WIDTH ** (-0.5)

    rows_in = jnp.concatenate(row_gather(stream), axis=1)
    gains = jnp.concatenate(row_gather(jnp.stack([first_gain, second_gain])), axis=1)
    gain1 = gains[0]
    gain2 = gains[1]

    def heads_of(blocks, h):
        return lax.dynamic_index_in_dim(blocks, (col - h) % N, 0, keepdims=False)

    wq_col = jnp.stack(col_gather(query_weight))
    wq = jnp.concatenate(row_exchange(lambda j: heads_of(wq_col, row ^ j)), axis=0)
    kv_all = jnp.concatenate(
        [
            key_weight.reshape(feat, KEY_VALUE_HEADS, 1, HEAD_WIDTH),
            value_weight.reshape(feat, KEY_VALUE_HEADS, 1, HEAD_WIDTH),
        ],
        axis=2,
    ).reshape(feat, N, HEAD_WIDTH)
    kv_all = jnp.transpose(kv_all, (1, 0, 2))
    kv_bias = jnp.stack(
        [key_bias.reshape(KEY_VALUE_HEADS, HEAD_WIDTH), value_bias.reshape(KEY_VALUE_HEADS, HEAD_WIDTH)],
        axis=1,
    ).reshape(N, HEAD_WIDTH)

    def kind_of(blocks, h):
        return lax.dynamic_index_in_dim(blocks, h, 0, keepdims=False)

    wkv = jnp.concatenate(row_exchange(lambda j: kind_of(kv_all, row ^ j)), axis=0)
    bkv = kind_of(kv_bias, row)
    bq = heads_of(jnp.stack(col_gather(query_bias)), row)
    wo_col = jnp.stack(col_gather(output_weight))
    wo = jnp.concatenate(row_exchange(lambda j: heads_of(wo_col, row ^ j)), axis=1)

    source = rows_in.astype(f32)
    scale1 = lax.rsqrt(jnp.sum(source * source, axis=1, keepdims=True) / width + epsilon)
    normed1 = (source * scale1 * gain1[None, :]).astype(bf16)

    units = seq_units[0]
    place = col * tok + jnp.arange(tok, dtype=jnp.int32)
    seg_q, pos = layout_of(place, units)
    half = HEAD_WIDTH // 2
    frequency = rope_base ** (-jnp.arange(half, dtype=f32) / half)
    angle = pos.astype(f32)[:, None] * frequency[None, :]
    cosine = jnp.cos(angle)
    sine = jnp.sin(angle)
    cos_kv = jnp.where(core == 0, cosine, 1.0)
    sin_kv = jnp.where(core == 0, sine, 0.0)

    kv_here = rotate(dot(normed1, wkv, 1, 0) + bkv[None, :], cos_kv, sin_kv).astype(bf16)
    kv_mine = jnp.concatenate([kv_here, zstep(kv_here, 1), zstep(kv_here, 2)], axis=0)
    kv_other = rowx(kv_mine, 1)
    keys = jnp.where(core == 0, kv_mine, kv_other)
    values = jnp.where(core == 0, kv_other, kv_mine)

    q = (dot(normed1, wq, 1, 0) + bq[None, :]).reshape(tok, heads, HEAD_WIDTH)
    queries = rotate(q, cosine[:, None, :], sine[:, None, :]).astype(bf16)

    key_place = jnp.concatenate([place, place - tok, place - 2 * tok])
    seg_k, _ = layout_of(key_place, units)
    mask = (
        (seg_q[:, None] == seg_k[None, :])
        & (key_place[None, :] <= place[:, None])
        & (key_place[None, :] >= 0)
    )
    scores = jnp.einsum("qhd,kd->hqk", queries, keys, preferred_element_type=f32) * scale_qk
    scores = jnp.where(mask[None], scores, neg_large)
    peak = jnp.max(scores, axis=2, keepdims=True)
    log_total = peak + jnp.log(jnp.sum(jnp.exp(scores - peak), axis=2, keepdims=True))
    prob_full = jnp.exp(scores - log_total)
    probs = prob_full.astype(bf16)
    attended = jnp.einsum("hqk,kd->qhd", probs, values, preferred_element_type=f32)
    attended = attended.astype(bf16).reshape(tok, heads * HEAD_WIDTH)

    proj = dot(attended, wo, 1, 0).astype(bf16)
    proj = [proj[:, j * feat : (j + 1) * feat] for j in range(N)]
    second_own = stream.astype(f32) + row_scatter(proj)

    def slices(weight):
        return weight.reshape(N, slice_width, feat)

    def all_d(weight):
        blocks = slices(weight)
        return jnp.concatenate(row_exchange(lambda j: kind_of(blocks, row ^ j)), axis=1)

    gate_t = all_d(gate_weight.T)
    up_t = all_d(up_weight.T)
    down = all_d(down_weight)

    cot_blocks = [jnp.concatenate(row_gather(z), axis=1) for z in col_gather(cotangent)]
    cot = jnp.concatenate(cot_blocks, axis=0)

    second_blocks = [
        jnp.concatenate(row_gather(z), axis=1) for z in col_gather(second_own.astype(bf16))
    ]
    second = jnp.concatenate(second_blocks, axis=0).astype(f32)
    scale2 = lax.rsqrt(jnp.sum(second * second, axis=1, keepdims=True) / width + epsilon)
    normed2 = (second * scale2 * gain2[None, :]).astype(bf16)
    gate_pre = dot(normed2, gate_t, 1, 1)
    up_pre = dot(normed2, up_t, 1, 1)
    hidden_grad = dot(cot, down, 1, 1)
    sigma = jax.nn.sigmoid(gate_pre)
    hidden = (gate_pre * sigma * up_pre).astype(bf16)
    gate_grad = (hidden_grad * up_pre * sigma * (1.0 + gate_pre * (1.0 - sigma))).astype(bf16)
    up_grad = (hidden_grad * gate_pre * sigma).astype(bf16)

    def block_scatter(partial):
        p = partial.reshape(N, tok, N, feat)
        parts = []
        for i in range(N):
            q0 = p[i, :, 0].astype(f32) + rowx(p[i, :, 1], 1).astype(f32)
            q2 = p[i, :, 2].astype(f32) + rowx(p[i, :, 3], 1).astype(f32)
            parts.append((q0 + rowx(q2.astype(bf16), 2).astype(f32)).astype(bf16))
        return col_scatter(parts)

    normed2_partial = (dot(gate_grad, gate_t, 1, 0) + dot(up_grad, up_t, 1, 0)).astype(bf16)
    normed2_grad = block_scatter(normed2_partial)
    down_own = block_scatter(dot(hidden, down, 1, 0).astype(bf16))
    block_out = (second_own + down_own).astype(bf16)

    def weight_reduce(grad):
        g = grad.astype(bf16)
        if n_dp == 2:
            part = slice_width // 2
            g = g.reshape(2, part, width)
            keep = lax.dynamic_index_in_dim(g, rep, 0, keepdims=False)
            give = lax.dynamic_index_in_dim(g, 1 - rep, 0, keepdims=False)
            got = lax.ppermute(give, "dp", [(0, 1), (1, 0)])
            g = (keep.astype(f32) + got.astype(f32)).astype(bf16)
        else:
            part = slice_width
            g = lax.psum(g, "dp")
        blocks = row_exchange(lambda j: g[:, j * feat : (j + 1) * feat])
        blocks = xor_order(blocks, core, yy)
        whole = jnp.stack(blocks)
        if n_dp == 2:
            far = lax.ppermute(whole, "dp", [(0, 1), (1, 0)])
            low = jnp.where(rep == 0, whole, far)
            high = jnp.where(rep == 0, far, whole)
            whole = jnp.stack([low, high], axis=1)
        return whole.reshape(hidden_width, feat)

    down_weight_grad = weight_reduce(dot(hidden, cot, 0, 0)).astype(f32)
    gate_weight_grad = weight_reduce(dot(gate_grad, normed2, 0, 0)).T.astype(f32)
    up_weight_grad = weight_reduce(dot(up_grad, normed2, 0, 0)).T.astype(f32)

    grad_rows = jnp.concatenate(row_gather(normed2_grad.astype(bf16)), axis=1).astype(f32)
    unit2 = second[:tok] * scale2[:tok]
    w = grad_rows * gain2[None, :]
    inner = jnp.sum(w * unit2, axis=1, keepdims=True) / width
    second_grad = cot_blocks[0].astype(f32) + scale2[:tok] * (w - unit2 * inner)
    mixed = second_grad.astype(bf16)
    second_grad_own = second_grad[:, :feat]
    second_gain_part = jnp.sum(grad_rows[:, :feat] * unit2[:, :feat], axis=0)

    attended_grad = dot(mixed, wo, 1, 1).astype(bf16)
    out_slab = attended_grad.reshape(tok, heads, HEAD_WIDTH)
    attn_slab = attended.reshape(tok, heads, HEAD_WIDTH)
    value_term = jnp.einsum("hqk,qhd->kd", probs, out_slab, preferred_element_type=f32)
    prob_grad = jnp.einsum("qhd,kd->hqk", out_slab, values, preferred_element_type=f32)
    delta = jnp.sum(out_slab.astype(f32) * attn_slab.astype(f32), axis=2)
    score_grad = (prob_full * (prob_grad - jnp.transpose(delta)[:, :, None]) * scale_qk).astype(bf16)
    query_raw = jnp.einsum("hqk,kd->qhd", score_grad, keys, preferred_element_type=f32)
    key_term = jnp.einsum("hqk,qhd->kd", score_grad, queries, preferred_element_type=f32)

    query_grad = rotate(query_raw, cosine[:, None, :], -sine[:, None, :]).astype(bf16)
    query_grad = query_grad.reshape(tok, heads * HEAD_WIDTH)
    kept = jnp.where(core == 0, key_term, value_term)
    given = jnp.where(core == 0, value_term, key_term)
    kept = (kept + rowx(given.astype(bf16), 1).astype(f32)).astype(bf16)
    back1 = zstep(kept[tok : 2 * tok], -1)
    back2 = zstep(kept[2 * tok :], -2)
    kv_raw = kept[:tok].astype(f32) + back1.astype(f32) + back2.astype(f32)
    kv_grad = rotate(kv_raw, cos_kv, -sin_kv).astype(bf16)

    normed1_part = dot(query_grad, wq, 1, 1) + dot(kv_grad, wkv, 1, 1)
    unit1 = source * scale1
    inner_part = jnp.sum(normed1_part * (gain1[None, :] * unit1), axis=1)
    inner1 = inner_part + rowx(inner_part, 1)
    inner1 = (inner1 + rowx(inner1, 2)) / width
    normed1_part = normed1_part.astype(bf16)
    normed1_grad = row_scatter([normed1_part[:, j * feat : (j + 1) * feat] for j in range(N)])
    unit1_own = unit1[:, :feat]
    w1 = normed1_grad * gain1[None, :feat]
    input_grad = second_grad_own + scale1 * (w1 - unit1_own * inner1[:, None])
    input_grad = input_grad.astype(bf16)
    first_gain_part = jnp.sum(normed1_grad * unit1_own, axis=0)

    normed1_col = jnp.concatenate(col_gather(normed1[:, :feat]), axis=0)
    mixed_col = jnp.concatenate(col_gather(mixed[:, :feat]), axis=0)
    attended_diag = jnp.concatenate(diagonal_gather(attended, row, col), axis=0)
    query_diag = jnp.concatenate(diagonal_gather(query_grad, row, col), axis=0)
    output_weight_grad = dp_sum(dot(attended_diag, mixed_col, 0, 0))
    query_weight_grad = dp_sum(dot(normed1_col, query_diag, 0, 0))
    query_bias_grad = jnp.sum(query_diag.astype(f32), axis=0)

    kv_rel = jnp.stack([jnp.stack(row_gather(z)) for z in col_gather(kv_grad)])
    kv_rel = jnp.stack(xor_order([kv_rel[:, j] for j in range(N)], core, yy), axis=2)
    order = (col - jnp.arange(N, dtype=jnp.int32)) % N
    kv_abs = jnp.take(kv_rel, order, axis=0).reshape(N * tok, N * HEAD_WIDTH)
    normed1_abs = jnp.take(normed1_col.reshape(N, tok, feat), order, axis=0).reshape(N * tok, feat)
    kv_weight_grad = dp_sum(dot(normed1_abs, kv_abs, 0, 0))
    kv_weight_grad = kv_weight_grad.reshape(feat, KEY_VALUE_HEADS, 2, HEAD_WIDTH)
    key_weight_grad = kv_weight_grad[:, :, 0].reshape(feat, KEY_VALUE_HEADS * HEAD_WIDTH)
    value_weight_grad = kv_weight_grad[:, :, 1].reshape(feat, KEY_VALUE_HEADS * HEAD_WIDTH)
    kv_bias_grad = jnp.sum(kv_abs.astype(f32), axis=0)

    small = jnp.stack([second_gain_part, first_gain_part])
    small = small + lax.ppermute(small, "col", [(i, i ^ 1) for i in range(N)])
    small = small + lax.ppermute(small, "col", [(i, i ^ 2) for i in range(N)])
    small = jnp.concatenate([small.reshape(-1), query_bias_grad, kv_bias_grad])
    if n_dp == 2:
        small = small + lax.ppermute(small, "dp", [(0, 1), (1, 0)])
    else:
        small = lax.psum(small, "dp")
    second_gain_grad = small[:feat]
    first_gain_grad = small[feat : 2 * feat]
    query_bias_grad = small[2 * feat : 2 * feat + heads * HEAD_WIDTH]
    kv_bias_grad = small[2 * feat + heads * HEAD_WIDTH :].reshape(KEY_VALUE_HEADS, 2, HEAD_WIDTH)
    key_bias_grad = kv_bias_grad[:, 0].reshape(-1)
    value_bias_grad = kv_bias_grad[:, 1].reshape(-1)
    return (
        block_out,
        input_grad,
        first_gain_grad,
        query_weight_grad,
        query_bias_grad,
        key_weight_grad,
        key_bias_grad,
        value_weight_grad,
        value_bias_grad,
        output_weight_grad,
        second_gain_grad,
        gate_weight_grad,
        up_weight_grad,
        down_weight_grad,
    )


def solution(mesh):
    placed = (
        P(("dp", "col"), "row"),
        P(("dp", "col"), "row"),
        P("row"),
        P("row", "col"),
        P("col"),
        P("row", None),
        P(),
        P("row", None),
        P(),
        P("col", "row"),
        P("row"),
        P("row", "col"),
        P("row", "col"),
        P("col", "row"),
        P("dp", None),
    )
    return jax.shard_map(
        local,
        mesh=mesh,
        in_specs=placed,
        out_specs=(
            P(("dp", "col"), "row"),
            P(("dp", "col"), "row"),
            P("row"),
            P("row", "col"),
            P("col"),
            P("row", None),
            P(),
            P("row", None),
            P(),
            P("col", "row"),
            P("row"),
            P("row", "col"),
            P("row", "col"),
            P("col", "row"),
        ),
        check_vma=False,
    )
```
